32 devices in a mesh: band: 4 (over y, x), query: 8 (over z, core).
Axes of the slice: x: 2, y: 2, z: 4, core: 2. Of those that a mesh axis runs over, the one named last changes fastest.
Arguments:
- spectra: bfloat16 [192, 20480], P('band'), may hold values from 0 to 3
- theo: bfloat16 [8, 8, 20480], P('query', 'band'), may hold values from -0.0390625 to 0.0390625
- offsets: int32 [16], replicated, may hold values from -128 to 128
- win_lo: int32 [192], P('band'), may hold values from 0 to 32
- win_len: int32 [192], P('band'), may hold values from 1 to 32
Outputs:
- best: float32 [192, 16], P(('band', 'query'))
- average: float32 [192, 16], P(('band', 'query'))
The draws below stay inside these ranges and needn't reach their ends.
Inputs may be any that keep to these rules, and one draw needn't show every extreme that they name: win_lo + win_len never exceeds 64.
All inputs are finite; a program needn't handle non-finite values.
Results may differ from the reference program's by a relative error of at most 0.003.
Values may be sent and summed in bfloat16 or wider, within the bound.
A program may use at most 128 MiB of HBM per device.

```python
import jax
import jax.numpy as jnp
from jax import lax

BINS = 20480
SHIFTS = 16
BG_HALF = 75
SHIFT_MAX = 128
GP = 8
PEPS = 64
SPECTRA = 192
WIN_MAX = 32
N_QUERY = 8


def place_ends(values, stream_key, smallest, largest):
    longest = values.shape.index(max(values.shape))
    spots = []
    for shift in (0, 1):
        where = [jax.random.randint(jax.random.fold_in(stream_key, axis), (), 0, length) for axis, length in enumerate(values.shape)]
        where[longest] = (where[longest] + shift) % values.shape[longest]
        spots.append(tuple(where))
    return values.at[spots[0]].set(smallest).at[spots[1]].set(largest)


def steps_of(key, shape, pieces, smallest, largest):
    gain = 1.0
    for position, shards_of in pieces:
        draws = jax.random.uniform(jax.random.fold_in(jax.random.fold_in(key, 6), position), (shards_of,), jnp.float32, smallest / len(pieces), largest / len(pieces))
        gain = gain * jnp.repeat(jnp.exp(draws), shape[position] // shards_of).reshape((-1,) + (1,) * (len(shape) - 1 - position))
    return gain


def gaussian(key, extent, scale, bound, split=(), kind=jnp.bfloat16):
    level = steps_of(key, extent, split, -0.22, 0.18) if split else 1.0
    result = jax.random.normal(key, extent, jnp.float32) * scale * level
    return jnp.minimum(jnp.maximum(result, -bound), bound).astype(kind)


def setup_inputs(seed: int = 0) -> dict:
    streams_of = jax.random.split(jax.random.key(seed), 6)
    return {
        "spectra": jnp.clip(3.0 * jax.random.uniform(streams_of[0], (SPECTRA, BINS), jnp.float32) ** steps_of(streams_of[0], (SPECTRA, BINS), ((0, 4),), -0.2, 0.2), 0.0, 3.0).astype(jnp.bfloat16),
        "theo": gaussian(streams_of[1], (N_QUERY, GP, BINS), BINS ** -0.5, 0.0390625, ((0, 8), (1, 4))),
        "offsets": place_ends(jax.random.randint(streams_of[2], (SHIFTS,), 0 - SHIFT_MAX, SHIFT_MAX + 1), jax.random.fold_in(streams_of[2], 1), 0 - SHIFT_MAX, SHIFT_MAX).astype(jnp.int32),
        "win_lo": place_ends(jax.random.randint(streams_of[3], (SPECTRA,), 0, PEPS - WIN_MAX + 1), jax.random.fold_in(streams_of[3], 1), 0, PEPS - WIN_MAX).astype(jnp.int32),
        "win_len": place_ends(jax.random.randint(streams_of[4], (SPECTRA,), 1, WIN_MAX + 1), jax.random.fold_in(streams_of[4], 1), 1, WIN_MAX).astype(jnp.int32),
    }


def reference(spectra, theo, offsets, win_lo, win_len):
    intensity = spectra.astype(jnp.float32)
    padded = jnp.pad(intensity, ((0, 0), (BG_HALF, BG_HALF)))
    window_sum = lax.reduce_window(padded, jnp.float32(0.0), lax.add, (1, 2 * BG_HALF + 1), (1, 1), "VALID")
    box_sum = window_sum - intensity
    corrected = (intensity - box_sum / (2.0 * BG_HALF)).astype(jnp.bfloat16)
    corrected_pad = jnp.pad(corrected.astype(jnp.float32), ((0, 0), (SHIFT_MAX, SHIFT_MAX)))
    peptide_rows = theo.reshape(PEPS, BINS).astype(jnp.float32)

    def one_shift(offset):
        shifted = lax.dynamic_slice_in_dim(corrected_pad, (SHIFT_MAX + offset).astype(jnp.int32), BINS, 1)
        return jnp.dot(shifted, peptide_rows.T, preferred_element_type=jnp.float32, precision=lax.Precision.HIGHEST)

    scores = lax.map(one_shift, offsets)
    peptide_index = jnp.arange(PEPS, dtype=jnp.int32)
    inside = (peptide_index[None, :] >= win_lo[:, None]) & (peptide_index[None, :] < (win_lo + win_len)[:, None])
    best_score = jnp.max(jnp.where(inside[None], scores, -jnp.inf), axis=2).T
    totals = jnp.sum(jnp.where(inside[None], scores, jnp.float32(0.0)), axis=2).T
    average = totals / win_len[:, None].astype(jnp.float32)
    return best_score, average
```

```python
import functools

import jax
import jax.numpy as jnp
from jax import lax
from jax.experimental import pallas as pl
from jax.experimental.pallas import tpu as pltpu
from jax.sharding import PartitionSpec as P

BG_HALF = 75
SHIFT_MAX = 128
LANES = 128
BLOCK = 256
BOX_BLOCKS = 16
CUTS = (5, 10, 15, 20)
MESH = pl.DeviceIdType.MESH


def box_tables():
    row = lax.broadcasted_iota(jnp.int32, (BLOCK, BLOCK), 0)
    target = lax.broadcasted_iota(jnp.int32, (BLOCK, BLOCK), 1)
    gap = row - target
    middle = (jnp.abs(gap) <= BG_HALF) & (gap != 0)
    side_gap = jnp.where(row < LANES, row - LANES, row + LANES) - target
    side = jnp.abs(side_gap) <= BG_HALF
    return middle.astype(jnp.float32).astype(jnp.bfloat16), side.astype(jnp.float32).astype(jnp.bfloat16)


def other(i, me):
    return i + (i >= me).astype(jnp.int32)


def kernel(
    nb, nq,
    spectra_ref, theo_ref, offsets_hbm, lo_hbm, len_hbm,
    out_ref,
    spec, corr, gathered, pairs, sums, tables, send, recv,
    offsets_ref, lo_ref, len_ref, small_sem, spec_sem, own_sem, band_send, band_recv, query_send, query_recv,
):
    rows, bins = spectra_ref.shape
    peps = theo_ref.shape[1]
    shifts = offsets_hbm.shape[0]
    own = rows // nq
    blocks = bins // LANES
    per_chunk = 8 // peps
    chunks = nb * peps // 8
    width = BLOCK * BOX_BLOCKS
    box_steps = bins // width
    band = lax.axis_index("band")
    query = lax.axis_index("query")
    cuts = [0] + [blocks * cut // CUTS[-1] // 8 * 8 for cut in CUTS]
    parts = len(CUTS)

    barrier = pltpu.get_barrier_semaphore()
    for d in range(1, nb):
        pl.semaphore_signal(barrier, inc=1, device_id={"band": lax.rem(band + d, nb)}, device_id_type=MESH)
    for d in range(1, nq):
        pl.semaphore_signal(barrier, inc=1, device_id={"query": lax.rem(query + d, nq)}, device_id_type=MESH)

    def spec_copy(i):
        start = pl.multiple_of(i * width, width)
        return pltpu.make_async_copy(
            spectra_ref.at[:, pl.ds(start, width)],
            spec.at[:, pl.ds(pl.multiple_of(start + LANES, LANES), width)],
            spec_sem.at[i],
        )

    own_copy = pltpu.make_async_copy(theo_ref.at[0], gathered.at[band, :, pl.ds(0, bins)], own_sem)
    small = [
        pltpu.make_async_copy(source, target, small_sem.at[i])
        for i, (source, target) in enumerate(
            [(offsets_hbm, offsets_ref), (lo_hbm, lo_ref), (len_hbm, len_ref)]
        )
    ]

    def theo_copy(i, h):
        at = pl.ds(cuts[h] * LANES, (cuts[h + 1] - cuts[h]) * LANES)
        return pltpu.make_async_remote_copy(
            src_ref=theo_ref.at[0, :, at],
            dst_ref=gathered.at[band, :, at],
            send_sem=band_send.at[i, h],
            recv_sem=band_recv.at[band, h],
            device_id={"band": other(i, band)},
            device_id_type=MESH,
        )

    def theo_wait(i, h):
        at = pl.ds(cuts[h] * LANES, (cuts[h + 1] - cuts[h]) * LANES)
        source = other(i, band)
        pltpu.make_async_remote_copy(
            src_ref=theo_ref.at[0, :, at],
            dst_ref=gathered.at[source, :, at],
            send_sem=band_send.at[i, h],
            recv_sem=band_recv.at[source, h],
            device_id={"band": source},
            device_id_type=MESH,
        ).wait_recv()

    def local_start():
        for i in range(box_steps):
            spec_copy(i).start()
        own_copy.start()
        for copy in small:
            copy.start()

    local_start()
    pl.semaphore_wait(barrier, nb - 1 + nq - 1)
    for h in range(parts):
        for i in range(nb - 1):
            theo_copy(i, h).start()

    spec[:, :LANES] = jnp.zeros((rows, LANES), spec.dtype)
    spec[:, LANES + bins:] = jnp.zeros((rows, LANES), spec.dtype)
    tables[0], tables[1] = box_tables()
    send[...] = jnp.zeros_like(send)
    gathered[:, :, bins:] = jnp.zeros((nb, peps, LANES), gathered.dtype)
    for c in range(chunks):
        pairs[c, blocks + 1] = jnp.zeros((16, LANES), pairs.dtype)
    for copy in small:
        copy.wait()

    spec_copy(0).wait()

    @pl.loop(0, box_steps)
    def _(i):
        @pl.when(i + 1 < box_steps)
        def _():
            spec_copy(i + 1).wait()

        start = pl.multiple_of(i * width, width)
        middles, sides = [], []
        for j in range(BOX_BLOCKS):
            at = start + j * BLOCK
            before = spec[:, pl.ds(pl.multiple_of(at, LANES), LANES)]
            middles.append(spec[:, pl.ds(pl.multiple_of(at + LANES, LANES), BLOCK)])
            after = spec[:, pl.ds(pl.multiple_of(at + LANES + BLOCK, LANES), LANES)]
            sides.append(jnp.concatenate([before, after], axis=1))
        box = jnp.dot(jnp.concatenate(middles, axis=0), tables[0], preferred_element_type=jnp.float32)
        box += jnp.dot(jnp.concatenate(sides, axis=0), tables[1], preferred_element_type=jnp.float32)
        for j in range(BOX_BLOCKS):
            level = box[j * rows:(j + 1) * rows] * (1.0 / (2.0 * BG_HALF))
            fixed = middles[j].astype(jnp.float32) - level
            corr[:, pl.ds(pl.multiple_of(start + j * BLOCK, BLOCK), BLOCK)] = fixed.astype(jnp.bfloat16)

    own_copy.wait()
    lane = lax.broadcasted_iota(jnp.int32, (16, LANES), 1).astype(jnp.float32).astype(jnp.bfloat16)
    ahead = [SHIFT_MAX - offsets_ref[k] for k in range(shifts)]
    skip = [a // LANES for a in ahead]
    rest = [a % LANES for a in ahead]
    turn = [(LANES - r) % LANES for r in rest]
    edge = [jnp.full((16, LANES), r.astype(jnp.float32)).astype(jnp.bfloat16) for r in rest]
    wide = shifts * 16

    def read_blocks(c, first):
        at = pl.ds(pl.multiple_of(first * LANES, LANES), 9 * LANES)
        rows_of = [gathered[c * per_chunk + j, :, at].astype(jnp.float32) for j in range(per_chunk)]
        whole = jnp.concatenate(rows_of, axis=0)
        return [whole[:, t * LANES:(t + 1) * LANES] for t in range(9)]

    def pair(c, g):
        found = read_blocks(c, g * 8)
        for t in range(8):
            pairs[c, g * 8 + t + 1] = jnp.concatenate(found[t:t + 2], axis=0).astype(jnp.bfloat16)

    def span(c, first, last):
        columns, evens, odds = [], [], []
        for j in range(first, last, 2):
            turned = []
            for k in range(shifts):
                near = pairs[c, j + skip[k]]
                far = pairs[c, j + skip[k] + 1]
                turned.append(pltpu.roll(jnp.where(lane < edge[k], far, near), turn[k], 1))
            columns.append(jnp.concatenate(turned, axis=0))
            evens.append(corr[:, j * LANES:(j + 1) * LANES])
            odds.append(corr[:, (j + 1) * LANES:(j + 2) * LANES])
        shifted = jnp.concatenate(columns, axis=1)
        piece = jnp.concatenate(
            [jnp.concatenate(evens, axis=1), jnp.concatenate(odds, axis=1)], axis=0
        )
        return lax.dot_general(
            shifted, piece, (((1,), (1,)), ((), ())), preferred_element_type=jnp.float32
        )

    group_from = block_from = 0
    for h in range(parts):
        for i in range(nb - 1):
            theo_wait(i, h)
        if h < parts - 1:
            group_to = (cuts[h + 1] - 1) // 8
            block_to = (group_to * 8 - 1) // 4 * 4
        else:
            group_to, block_to = blocks // 8, blocks

        def work(c):
            if h == 0:
                start = read_blocks(c, 0)[0]
                pairs[c, 0] = jnp.concatenate([jnp.zeros_like(start), start], axis=0).astype(jnp.bfloat16)
            pl.loop(group_from, group_to, unroll=True)(functools.partial(pair, c))
            found = span(c, block_from, block_to)
            sums[c] = found if h == 0 else sums[c] + found

        if chunks == 1:
            work(0)
        else:
            pl.loop(0, chunks)(work)
        group_from, block_from = group_to, block_to

    row = lax.broadcasted_iota(jnp.int32, (8, rows), 0)
    lo = jnp.broadcast_to(lo_ref[...].reshape(1, rows), (8, rows))
    length = jnp.broadcast_to(len_ref[...].reshape(1, rows), (8, rows))
    best = [jnp.full((8, rows), -jnp.inf, jnp.float32)] * shifts
    total = [jnp.zeros((8, rows), jnp.float32)] * shifts
    for c in range(chunks):
        number = row + (query * (chunks * 8) + c * 8)
        inside = (number >= lo) & (number < lo + length)
        for k in range(shifts):
            scores = sums[c, 16 * k:16 * k + 8, :rows] + sums[c, 16 * k + 8:16 * k + 16, rows:]
            best[k] = jnp.maximum(best[k], jnp.where(inside, scores, -jnp.inf))
            total[k] = total[k] + jnp.where(inside, scores, 0.0)

    def fold(each, op):
        for reach in (4, 2, 1):
            upper = (row // reach) % 2 == 1
            merged = []
            for n in range(0, len(each), 2):
                moved = jnp.where(upper, each[n], each[n + 1])
                moved = jnp.where(upper, pltpu.roll(moved, reach, 0), pltpu.roll(moved, 8 - reach, 0))
                merged.append(op(jnp.where(upper, each[n + 1], each[n]), moved))
            each = merged
        return each[0]

    folded = []
    for each, op in ((best, jnp.maximum), (total, jnp.add)):
        for v in range(0, shifts, 8):
            folded.append(fold([each[v + k] for k in (0, 4, 2, 6, 1, 5, 3, 7)], op))
    whole = length.astype(jnp.float32)
    half = shifts // 8
    folded[half:] = [part / whole for part in folded[half:]]
    packed = jnp.concatenate(folded, axis=0).T
    for q in range(nq):
        send[q, :own, :2 * shifts] = packed[q * own:(q + 1) * own]

    def result_copy(i):
        target = other(i, query)
        return pltpu.make_async_remote_copy(
            src_ref=send.at[target],
            dst_ref=recv.at[query],
            send_sem=query_send.at[i],
            recv_sem=query_recv.at[query],
            device_id={"query": target},
            device_id_type=MESH,
        )

    def result_wait(i):
        source = other(i, query)
        pltpu.make_async_remote_copy(
            src_ref=send.at[source],
            dst_ref=recv.at[source],
            send_sem=query_send.at[i],
            recv_sem=query_recv.at[source],
            device_id={"query": source},
            device_id_type=MESH,
        ).wait_recv()

    for i in range(nq - 1):
        result_copy(i).start()
    mine = send[query]
    top, mean = mine, mine
    for i in range(nq - 1):
        result_wait(i)
        part = recv[other(i, query)]
        top = jnp.maximum(top, part)
        mean = mean + part
    out_ref[0] = top[:own, :shifts]
    out_ref[1] = pltpu.roll(mean, LANES - shifts, 1)[:own, :shifts]
    for h in range(parts):
        for i in range(nb - 1):
            theo_copy(i, h).wait_send()
    for i in range(nq - 1):
        result_copy(i).wait_send()


def local(spectra, theo, offsets, win_lo, win_len):
    nb, nq = lax.axis_size("band"), lax.axis_size("query")
    rows, bins = spectra.shape
    peps = theo.shape[1]
    shifts = offsets.shape[0]
    own = rows // nq
    slots = (own + 7) // 8 * 8
    chunks = nb * peps // 8
    placed = [pltpu.with_memory_space_constraint(x, pltpu.HBM) for x in (spectra, theo, offsets, win_lo, win_len)]
    both = pl.pallas_call(
        functools.partial(kernel, nb, nq),
        out_shape=pltpu.VMEM((2, own, shifts), jnp.float32),
        in_specs=[
            pl.BlockSpec(memory_space=pltpu.HBM),
        ] * 5,
        out_specs=pl.BlockSpec(memory_space=pltpu.VMEM),
        scratch_shapes=[
            pltpu.VMEM((rows, bins + 2 * LANES), jnp.bfloat16),
            pltpu.VMEM((rows, bins), jnp.bfloat16),
            pltpu.VMEM((nb, peps, bins + LANES), jnp.bfloat16),
            pltpu.VMEM((chunks, bins // LANES + 2, 16, LANES), jnp.bfloat16),
            pltpu.VMEM((chunks, 16 * shifts, 2 * rows), jnp.float32),
            pltpu.VMEM((2, BLOCK, BLOCK), jnp.bfloat16),
            pltpu.VMEM((nq, slots, LANES), jnp.float32),
            pltpu.VMEM((nq, slots, LANES), jnp.float32),
            pltpu.SMEM((shifts,), jnp.int32),
            pltpu.VMEM((rows,), jnp.int32),
            pltpu.VMEM((rows,), jnp.int32),
            pltpu.SemaphoreType.DMA((3,)),
            pltpu.SemaphoreType.DMA((bins // (BLOCK * BOX_BLOCKS),)),
            pltpu.SemaphoreType.DMA,
            pltpu.SemaphoreType.DMA((nb, len(CUTS))),
            pltpu.SemaphoreType.DMA((nb, len(CUTS))),
            pltpu.SemaphoreType.DMA((nq,)),
            pltpu.SemaphoreType.DMA((nq,)),
        ],
        compiler_params=pltpu.CompilerParams(
            collective_id=0, has_side_effects=True, vmem_limit_bytes=40 * 2**20
        ),
        name="shifted_scores",
    )(*placed)
    return both[0], both[1]


def solution(mesh):
    placed = (P("band", None), P("query", "band", None), P(), P("band"), P("band"))
    return jax.shard_map(
        local,
        mesh=mesh,
        in_specs=placed,
        out_specs=(P(("band", "query"), None), P(("band", "query"), None)),
        check_vma=False,
    )
```

```python
import functools

import jax
import jax.numpy as jnp
from jax import lax
from jax.experimental import pallas as pl
from jax.experimental.pallas import tpu as pltpu
from jax.sharding import PartitionSpec as P

BG_HALF = 75
SHIFT_MAX = 128
LANES = 128
BLOCK = 256
BOX_BLOCKS = 16
CUTS = (4, 12, 20)
MEET = 1
MESH = pl.DeviceIdType.MESH


def box_tables():
    row = lax.broadcasted_iota(jnp.int32, (BLOCK, BLOCK), 0)
    target = lax.broadcasted_iota(jnp.int32, (BLOCK, BLOCK), 1)
    gap = row - target
    middle = (jnp.abs(gap) <= BG_HALF) & (gap != 0)
    side_gap = jnp.where(row < LANES, row - LANES, row + LANES) - target
    side = jnp.abs(side_gap) <= BG_HALF
    return middle.astype(jnp.float32).astype(jnp.bfloat16), side.astype(jnp.float32).astype(jnp.bfloat16)


def other(i, me):
    return i + (i >= me).astype(jnp.int32)


def kernel(
    nb, nq,
    spectra_ref, theo_ref, offsets_hbm, lo_hbm, len_hbm,
    out_ref,
    spec, corr, gathered, pairs, sums, tables, send, recv,
    offsets_ref, lo_ref, len_ref, small_sem, spec_sem, own_sem, band_send, band_recv, query_send, query_recv, arrived, go,
):
    rows, bins = spectra_ref.shape
    peps = theo_ref.shape[1]
    shifts = offsets_hbm.shape[0]
    own = rows // nq
    blocks = bins // LANES
    per_chunk = 8 // peps
    chunks = nb * peps // 8
    width = BLOCK * BOX_BLOCKS
    box_steps = bins // width
    band = lax.axis_index("band")
    query = lax.axis_index("query")
    cuts = [0] + [blocks * cut // CUTS[-1] // 8 * 8 for cut in CUTS]
    parts = len(CUTS)

    last = nb - 1
    leads, closes = band == 0, band == last
    between = jnp.logical_not(leads | closes)
    barrier = pltpu.get_barrier_semaphore()

    def signal(semaphore, axis, index):
        pl.semaphore_signal(semaphore, inc=1, device_id={axis: index}, device_id_type=MESH)

    @pl.when(jnp.logical_not(closes))
    def _():
        signal(barrier, "band", last)

    @pl.when(leads)
    def _():
        for b in range(1, last):
            signal(barrier, "band", b)

    def spec_copy(i):
        start = pl.multiple_of(i * width, width)
        return pltpu.make_async_copy(
            spectra_ref.at[:, pl.ds(start, width)],
            spec.at[:, pl.ds(pl.multiple_of(start + LANES, LANES), width)],
            spec_sem.at[i],
        )

    own_copy = pltpu.make_async_copy(theo_ref.at[0], gathered.at[band, :, pl.ds(0, bins)], own_sem)
    small = [
        pltpu.make_async_copy(source, target, small_sem.at[i])
        for i, (source, target) in enumerate(
            [(offsets_hbm, offsets_ref), (lo_hbm, lo_ref), (len_hbm, len_ref)]
        )
    ]

    def theo_copy(source, target, h):
        at = pl.ds(cuts[h] * LANES, (cuts[h + 1] - cuts[h]) * LANES)
        return pltpu.make_async_remote_copy(
            src_ref=theo_ref.at[0, :, at],
            dst_ref=gathered.at[source, :, at],
            send_sem=band_send.at[target, h],
            recv_sem=band_recv.at[source, h],
            device_id={"band": target},
            device_id_type=MESH,
        )

    def theo_start(targets):
        for h in range(parts):
            for target in targets:
                theo_copy(band, target, h).start()

    for i in range(box_steps):
        spec_copy(i).start()
    own_copy.start()
    for copy in small:
        copy.start()

    @pl.when(between)
    def _():
        pl.semaphore_wait(barrier, 1)
        signal(arrived.at[band], "band", 0)
        theo_start([0])

    @pl.when(closes)
    def _():
        pl.semaphore_wait(barrier, last)
        for b in range(last):
            signal(arrived.at[last], "band", b)
        theo_start(list(range(last)))


    @pl.when(between)
    def _():
        pl.semaphore_wait(arrived.at[last], 1)
        theo_start([last] + [other(i + 1, band) for i in range(nb - 3)])


    @pl.when(leads)
    def _():
        for b in range(1, nb):
            pl.semaphore_wait(arrived.at[b], 1)
        theo_start([last] + list(range(1, last)))
        for i in range(nq - 1):
            signal(barrier, "query", other(i, query))

    spec[:, :LANES] = jnp.zeros((rows, LANES), spec.dtype)
    spec[:, LANES + bins:] = jnp.zeros((rows, LANES), spec.dtype)
    tables[0], tables[1] = box_tables()
    send[...] = jnp.zeros_like(send)
    gathered[:, :, bins:] = jnp.zeros((nb, peps, LANES), gathered.dtype)
    for c in range(chunks):
        pairs[c, blocks + 1] = jnp.zeros((16, LANES), pairs.dtype)
    for copy in small:
        copy.wait()

    spec_copy(0).wait()

    @pl.loop(0, box_steps)
    def _(i):
        @pl.when(i + 1 < box_steps)
        def _():
            spec_copy(i + 1).wait()

        start = pl.multiple_of(i * width, width)
        middles, sides = [], []
        for j in range(BOX_BLOCKS):
            at = start + j * BLOCK
            before = spec[:, pl.ds(pl.multiple_of(at, LANES), LANES)]
            middles.append(spec[:, pl.ds(pl.multiple_of(at + LANES, LANES), BLOCK)])
            after = spec[:, pl.ds(pl.multiple_of(at + LANES + BLOCK, LANES), LANES)]
            sides.append(jnp.concatenate([before, after], axis=1))
        box = jnp.dot(jnp.concatenate(middles, axis=0), tables[0], preferred_element_type=jnp.float32)
        box += jnp.dot(jnp.concatenate(sides, axis=0), tables[1], preferred_element_type=jnp.float32)
        for j in range(BOX_BLOCKS):
            level = box[j * rows:(j + 1) * rows] * (1.0 / (2.0 * BG_HALF))
            fixed = middles[j].astype(jnp.float32) - level
            corr[:, pl.ds(pl.multiple_of(start + j * BLOCK, BLOCK), BLOCK)] = fixed.astype(jnp.bfloat16)

    own_copy.wait()
    lane = lax.broadcasted_iota(jnp.int32, (16, LANES), 1).astype(jnp.float32).astype(jnp.bfloat16)
    ahead = [SHIFT_MAX - offsets_ref[k] for k in range(shifts)]
    skip = [a // LANES for a in ahead]
    rest = [a % LANES for a in ahead]
    turn = [(LANES - r) % LANES for r in rest]
    edge = [jnp.full((16, LANES), r.astype(jnp.float32)).astype(jnp.bfloat16) for r in rest]
    wide = shifts * 16

    def read_blocks(c, first):
        at = pl.ds(pl.multiple_of(first * LANES, LANES), 9 * LANES)
        rows_of = [gathered[c * per_chunk + j, :, at].astype(jnp.float32) for j in range(per_chunk)]
        whole = jnp.concatenate(rows_of, axis=0)
        return [whole[:, t * LANES:(t + 1) * LANES] for t in range(9)]

    def pair(c, g):
        found = read_blocks(c, g * 8)
        for t in range(8):
            pairs[c, g * 8 + t + 1] = jnp.concatenate(found[t:t + 2], axis=0).astype(jnp.bfloat16)

    def span(c, first, last):
        columns, evens, odds = [], [], []
        for j in range(first, last, 2):
            turned = []
            for k in range(shifts):
                near = pairs[c, j + skip[k]]
                far = pairs[c, j + skip[k] + 1]
                turned.append(pltpu.roll(jnp.where(lane < edge[k], far, near), turn[k], 1))
            columns.append(jnp.concatenate(turned, axis=0))
            evens.append(corr[:, j * LANES:(j + 1) * LANES])
            odds.append(corr[:, (j + 1) * LANES:(j + 2) * LANES])
        shifted = jnp.concatenate(columns, axis=1)
        piece = jnp.concatenate(
            [jnp.concatenate(evens, axis=1), jnp.concatenate(odds, axis=1)], axis=0
        )
        return lax.dot_general(
            shifted, piece, (((1,), (1,)), ((), ())), preferred_element_type=jnp.float32
        )

    group_from = block_from = 0
    for h in range(parts):
        for i in range(nb - 1):
            theo_copy(other(i, band), other(i, band), h).wait_recv()
        if h < parts - 1:
            group_to = (cuts[h + 1] - 1) // 8
            block_to = (group_to * 8 - 1) // 4 * 4
        else:
            group_to, block_to = blocks // 8, blocks

        def work(c):
            if h == 0:
                start = read_blocks(c, 0)[0]
                pairs[c, 0] = jnp.concatenate([jnp.zeros_like(start), start], axis=0).astype(jnp.bfloat16)
            pl.loop(group_from, group_to, unroll=True)(functools.partial(pair, c))
            found = span(c, block_from, block_to)
            sums[c] = found if h == 0 else sums[c] + found

        if chunks == 1:
            work(0)
        else:
            pl.loop(0, chunks)(work)
        group_from, block_from = group_to, block_to

        if h == MEET:
            @pl.when(leads)
            def _():
                pl.semaphore_wait(barrier, nq - 1)
                for b in range(1, nb):
                    signal(go, "band", b)

    row = lax.broadcasted_iota(jnp.int32, (8, rows), 0)
    lo = jnp.broadcast_to(lo_ref[...].reshape(1, rows), (8, rows))
    length = jnp.broadcast_to(len_ref[...].reshape(1, rows), (8, rows))
    best = [jnp.full((8, rows), -jnp.inf, jnp.float32)] * shifts
    total = [jnp.zeros((8, rows), jnp.float32)] * shifts
    for c in range(chunks):
        number = row + (query * (chunks * 8) + c * 8)
        inside = (number >= lo) & (number < lo + length)
        for k in range(shifts):
            scores = sums[c, 16 * k:16 * k + 8, :rows] + sums[c, 16 * k + 8:16 * k + 16, rows:]
            best[k] = jnp.maximum(best[k], jnp.where(inside, scores, -jnp.inf))
            total[k] = total[k] + jnp.where(inside, scores, 0.0)

    def fold(each, op):
        for reach in (4, 2, 1):
            upper = (row // reach) % 2 == 1
            merged = []
            for n in range(0, len(each), 2):
                moved = jnp.where(upper, each[n], each[n + 1])
                moved = jnp.where(upper, pltpu.roll(moved, reach, 0), pltpu.roll(moved, 8 - reach, 0))
                merged.append(op(jnp.where(upper, each[n + 1], each[n]), moved))
            each = merged
        return each[0]

    folded = []
    for each, op in ((best, jnp.maximum), (total, jnp.add)):
        for v in range(0, shifts, 8):
            folded.append(fold([each[v + k] for k in (0, 4, 2, 6, 1, 5, 3, 7)], op))
    whole = length.astype(jnp.float32)
    half = shifts // 8
    folded[half:] = [part / whole for part in folded[half:]]
    packed = jnp.concatenate(folded, axis=0).T
    for q in range(nq):
        send[q, :own, :2 * shifts] = packed[q * own:(q + 1) * own]

    def result_copy(i):
        target = other(i, query)
        return pltpu.make_async_remote_copy(
            src_ref=send.at[target],
            dst_ref=recv.at[query],
            send_sem=query_send.at[i],
            recv_sem=query_recv.at[query],
            device_id={"query": target},
            device_id_type=MESH,
        )

    def result_wait(i):
        source = other(i, query)
        pltpu.make_async_remote_copy(
            src_ref=send.at[source],
            dst_ref=recv.at[source],
            send_sem=query_send.at[i],
            recv_sem=query_recv.at[source],
            device_id={"query": source},
            device_id_type=MESH,
        ).wait_recv()

    @pl.when(jnp.logical_not(leads))
    def _():
        pl.semaphore_wait(go, 1)

    for i in range(nq - 1):
        result_copy(i).start()
    for h in range(parts):
        for i in range(nb - 1):
            theo_copy(band, other(i, band), h).wait_send()
    for i in range(nq - 1):
        result_copy(i).wait_send()
    mine = send[query]
    top, mean = mine, mine
    for i in range(nq - 1):
        result_wait(i)
        part = recv[other(i, query)]
        top = jnp.maximum(top, part)
        mean = mean + part
    out_ref[0] = top[:own, :shifts]
    out_ref[1] = pltpu.roll(mean, LANES - shifts, 1)[:own, :shifts]


def local(spectra, theo, offsets, win_lo, win_len):
    nb, nq = lax.axis_size("band"), lax.axis_size("query")
    rows, bins = spectra.shape
    peps = theo.shape[1]
    shifts = offsets.shape[0]
    own = rows // nq
    slots = (own + 7) // 8 * 8
    chunks = nb * peps // 8
    placed = [pltpu.with_memory_space_constraint(x, pltpu.HBM) for x in (spectra, theo, offsets, win_lo, win_len)]
    both = pl.pallas_call(
        functools.partial(kernel, nb, nq),
        out_shape=pltpu.VMEM((2, own, shifts), jnp.float32),
        in_specs=[
            pl.BlockSpec(memory_space=pltpu.HBM),
        ] * 5,
        out_specs=pl.BlockSpec(memory_space=pltpu.VMEM),
        scratch_shapes=[
            pltpu.VMEM((rows, bins + 2 * LANES), jnp.bfloat16),
            pltpu.VMEM((rows, bins), jnp.bfloat16),
            pltpu.VMEM((nb, peps, bins + LANES), jnp.bfloat16),
            pltpu.VMEM((chunks, bins // LANES + 2, 16, LANES), jnp.bfloat16),
            pltpu.VMEM((chunks, 16 * shifts, 2 * rows), jnp.float32),
            pltpu.VMEM((2, BLOCK, BLOCK), jnp.bfloat16),
            pltpu.VMEM((nq, slots, LANES), jnp.float32),
            pltpu.VMEM((nq, slots, LANES), jnp.float32),
            pltpu.SMEM((shifts,), jnp.int32),
            pltpu.VMEM((rows,), jnp.int32),
            pltpu.VMEM((rows,), jnp.int32),
            pltpu.SemaphoreType.DMA((3,)),
            pltpu.SemaphoreType.DMA((bins // (BLOCK * BOX_BLOCKS),)),
            pltpu.SemaphoreType.DMA,
            pltpu.SemaphoreType.DMA((nb, len(CUTS))),
            pltpu.SemaphoreType.DMA((nb, len(CUTS))),
            pltpu.SemaphoreType.DMA((nq,)),
            pltpu.SemaphoreType.DMA((nq,)),
            pltpu.SemaphoreType.REGULAR((nb,)),
            pltpu.SemaphoreType.REGULAR,
        ],
        compiler_params=pltpu.CompilerParams(
            collective_id=0, has_side_effects=True, vmem_limit_bytes=40 * 2**20
        ),
        name="shifted_scores",
    )(*placed)
    return both[0], both[1]


def solution(mesh):
    placed = (P("band", None), P("query", "band", None), P(), P("band"), P("band"))
    return jax.shard_map(
        local,
        mesh=mesh,
        in_specs=placed,
        out_specs=(P(("band", "query"), None), P(("band", "query"), None)),
        check_vma=False,
    )
```

```python
import functools

import jax
import jax.numpy as jnp
from jax import lax
from jax.experimental import pallas as pl
from jax.experimental.pallas import tpu as pltpu
from jax.sharding import PartitionSpec as P

BG_HALF = 75
SHIFT_MAX = 128
LANES = 128
BLOCK = 256
BOX_BLOCKS = 16
CUTS = (2, 8, 20)
MEET = 1
MESH = pl.DeviceIdType.MESH


def box_tables():
    row = lax.broadcasted_iota(jnp.int32, (BLOCK, BLOCK), 0)
    target = lax.broadcasted_iota(jnp.int32, (BLOCK, BLOCK), 1)
    gap = row - target
    middle = (jnp.abs(gap) <= BG_HALF) & (gap != 0)
    side_gap = jnp.where(row < LANES, row - LANES, row + LANES) - target
    side = jnp.abs(side_gap) <= BG_HALF
    return middle.astype(jnp.float32).astype(jnp.bfloat16), side.astype(jnp.float32).astype(jnp.bfloat16)


def other(i, me):
    return i + (i >= me).astype(jnp.int32)


def kernel(
    nb, nq,
    spectra_ref, theo_ref, offsets_hbm, lo_hbm, len_hbm,
    out_ref,
    spec, corr, gathered, pairs, sums, tables, send, recv,
    offsets_ref, lo_ref, len_ref, small_sem, spec_sem, own_sem, band_send, band_recv, query_send, query_recv, arrived, go,
):
    rows, bins = spectra_ref.shape
    peps = theo_ref.shape[1]
    shifts = offsets_hbm.shape[0]
    own = rows // nq
    blocks = bins // LANES
    per_chunk = 8 // peps
    chunks = nb * peps // 8
    width = BLOCK * BOX_BLOCKS
    box_steps = bins // width
    band = lax.axis_index("band")
    query = lax.axis_index("query")
    cuts = [0] + [blocks * cut // CUTS[-1] // 8 * 8 for cut in CUTS]
    parts = len(CUTS)

    last = nb - 1
    leads, closes = band == 0, band == last
    between = jnp.logical_not(leads | closes)
    barrier = pltpu.get_barrier_semaphore()

    def signal(semaphore, axis, index):
        pl.semaphore_signal(semaphore, inc=1, device_id={axis: index}, device_id_type=MESH)

    @pl.when(jnp.logical_not(closes))
    def _():
        signal(barrier, "band", last)

    @pl.when(leads)
    def _():
        for b in range(1, last):
            signal(barrier, "band", b)

    def spec_copy(i):
        start = pl.multiple_of(i * width, width)
        return pltpu.make_async_copy(
            spectra_ref.at[:, pl.ds(start, width)],
            spec.at[:, pl.ds(pl.multiple_of(start + LANES, LANES), width)],
            spec_sem.at[i],
        )

    own_copy = pltpu.make_async_copy(theo_ref.at[0], gathered.at[band, :, pl.ds(0, bins)], own_sem)
    small = [
        pltpu.make_async_copy(source, target, small_sem.at[i])
        for i, (source, target) in enumerate(
            [(offsets_hbm, offsets_ref), (lo_hbm, lo_ref), (len_hbm, len_ref)]
        )
    ]

    def theo_copy(source, target, h):
        at = pl.ds(cuts[h] * LANES, (cuts[h + 1] - cuts[h]) * LANES)
        return pltpu.make_async_remote_copy(
            src_ref=theo_ref.at[0, :, at],
            dst_ref=gathered.at[source, :, at],
            send_sem=band_send.at[target, h],
            recv_sem=band_recv.at[source, h],
            device_id={"band": target},
            device_id_type=MESH,
        )

    def theo_start(targets):
        for h in range(parts):
            for target in targets:
                theo_copy(band, target, h).start()

    for i in range(box_steps):
        spec_copy(i).start()
    own_copy.start()
    for copy in small:
        copy.start()

    @pl.when(between)
    def _():
        pl.semaphore_wait(barrier, 1)
        signal(arrived.at[band], "band", 0)
        theo_start([0])

    @pl.when(closes)
    def _():
        pl.semaphore_wait(barrier, last)
        for b in range(last):
            signal(arrived.at[last], "band", b)
        theo_start(list(range(last - 1)))


    @pl.when(between)
    def _():
        pl.semaphore_wait(arrived.at[last], 1)
        theo_start([last] + [other(i + 1, band) for i in range(nb - 3)])


    @pl.when(leads)
    def _():
        for b in range(1, last):
            pl.semaphore_wait(arrived.at[b], 1)
        theo_start(list(range(1, last)))
        pl.semaphore_wait(arrived.at[last], 1)
        theo_start([last])
        for i in range(nq - 1):
            signal(barrier, "query", other(i, query))

    spec[:, :LANES] = jnp.zeros((rows, LANES), spec.dtype)
    spec[:, LANES + bins:] = jnp.zeros((rows, LANES), spec.dtype)
    tables[0], tables[1] = box_tables()
    send[...] = jnp.zeros_like(send)
    gathered[:, :, bins:] = jnp.zeros((nb, peps, LANES), gathered.dtype)
    for c in range(chunks):
        pairs[c, blocks + 1] = jnp.zeros((16, LANES), pairs.dtype)
    for copy in small:
        copy.wait()

    spec_copy(0).wait()

    @pl.when(closes)
    def _():
        theo_start([last - 1])

    @pl.loop(0, box_steps)
    def _(i):
        @pl.when(i + 1 < box_steps)
        def _():
            spec_copy(i + 1).wait()

        start = pl.multiple_of(i * width, width)
        middles, sides = [], []
        for j in range(BOX_BLOCKS):
            at = start + j * BLOCK
            before = spec[:, pl.ds(pl.multiple_of(at, LANES), LANES)]
            middles.append(spec[:, pl.ds(pl.multiple_of(at + LANES, LANES), BLOCK)])
            after = spec[:, pl.ds(pl.multiple_of(at + LANES + BLOCK, LANES), LANES)]
            sides.append(jnp.concatenate([before, after], axis=1))
        box = jnp.dot(jnp.concatenate(middles, axis=0), tables[0], preferred_element_type=jnp.float32)
        box += jnp.dot(jnp.concatenate(sides, axis=0), tables[1], preferred_element_type=jnp.float32)
        for j in range(BOX_BLOCKS):
            level = box[j * rows:(j + 1) * rows] * (1.0 / (2.0 * BG_HALF))
            fixed = middles[j].astype(jnp.float32) - level
            corr[:, pl.ds(pl.multiple_of(start + j * BLOCK, BLOCK), BLOCK)] = fixed.astype(jnp.bfloat16)

    own_copy.wait()
    lane = lax.broadcasted_iota(jnp.int32, (16, LANES), 1).astype(jnp.float32).astype(jnp.bfloat16)
    ahead = [SHIFT_MAX - offsets_ref[k] for k in range(shifts)]
    skip = [a // LANES for a in ahead]
    rest = [a % LANES for a in ahead]
    turn = [(LANES - r) % LANES for r in rest]
    edge = [jnp.full((16, LANES), r.astype(jnp.float32)).astype(jnp.bfloat16) for r in rest]
    wide = shifts * 16

    def read_blocks(c, first):
        at = pl.ds(pl.multiple_of(first * LANES, LANES), 9 * LANES)
        rows_of = [gathered[c * per_chunk + j, :, at].astype(jnp.float32) for j in range(per_chunk)]
        whole = jnp.concatenate(rows_of, axis=0)
        return [whole[:, t * LANES:(t + 1) * LANES] for t in range(9)]

    def pair(c, g):
        found = read_blocks(c, g * 8)
        for t in range(8):
            pairs[c, g * 8 + t + 1] = jnp.concatenate(found[t:t + 2], axis=0).astype(jnp.bfloat16)

    def span(c, first, last):
        columns, evens, odds = [], [], []
        for j in range(first, last, 2):
            turned = []
            for k in range(shifts):
                near = pairs[c, j + skip[k]]
                far = pairs[c, j + skip[k] + 1]
                turned.append(pltpu.roll(jnp.where(lane < edge[k], far, near), turn[k], 1))
            columns.append(jnp.concatenate(turned, axis=0))
            evens.append(corr[:, j * LANES:(j + 1) * LANES])
            odds.append(corr[:, (j + 1) * LANES:(j + 2) * LANES])
        shifted = jnp.concatenate(columns, axis=1)
        piece = jnp.concatenate(
            [jnp.concatenate(evens, axis=1), jnp.concatenate(odds, axis=1)], axis=0
        )
        return lax.dot_general(
            shifted, piece, (((1,), (1,)), ((), ())), preferred_element_type=jnp.float32
        )

    group_from = block_from = 0
    for h in range(parts):
        for i in range(nb - 1):
            theo_copy(other(i, band), other(i, band), h).wait_recv()
        if h < parts - 1:
            group_to = (cuts[h + 1] - 1) // 8
            block_to = (group_to * 8 - 1) // 4 * 4
        else:
            group_to, block_to = blocks // 8, blocks

        def work(c):
            if h == 0:
                start = read_blocks(c, 0)[0]
                pairs[c, 0] = jnp.concatenate([jnp.zeros_like(start), start], axis=0).astype(jnp.bfloat16)
            pl.loop(group_from, group_to, unroll=True)(functools.partial(pair, c))
            found = span(c, block_from, block_to)
            sums[c] = found if h == 0 else sums[c] + found

        if chunks == 1:
            work(0)
        else:
            pl.loop(0, chunks)(work)
        group_from, block_from = group_to, block_to

        if h == MEET:
            @pl.when(leads)
            def _():
                pl.semaphore_wait(barrier, nq - 1)
                for b in range(1, nb):
                    signal(go, "band", b)

    row = lax.broadcasted_iota(jnp.int32, (8, rows), 0)
    lo = jnp.broadcast_to(lo_ref[...].reshape(1, rows), (8, rows))
    length = jnp.broadcast_to(len_ref[...].reshape(1, rows), (8, rows))
    best = [jnp.full((8, rows), -jnp.inf, jnp.float32)] * shifts
    total = [jnp.zeros((8, rows), jnp.float32)] * shifts
    for c in range(chunks):
        number = row + (query * (chunks * 8) + c * 8)
        inside = (number >= lo) & (number < lo + length)
        for k in range(shifts):
            scores = sums[c, 16 * k:16 * k + 8, :rows] + sums[c, 16 * k + 8:16 * k + 16, rows:]
            best[k] = jnp.maximum(best[k], jnp.where(inside, scores, -jnp.inf))
            total[k] = total[k] + jnp.where(inside, scores, 0.0)

    def fold(each, op):
        for reach in (4, 2, 1):
            upper = (row // reach) % 2 == 1
            merged = []
            for n in range(0, len(each), 2):
                moved = jnp.where(upper, each[n], each[n + 1])
                moved = jnp.where(upper, pltpu.roll(moved, reach, 0), pltpu.roll(moved, 8 - reach, 0))
                merged.append(op(jnp.where(upper, each[n + 1], each[n]), moved))
            each = merged
        return each[0]

    folded = []
    for each, op in ((best, jnp.maximum), (total, jnp.add)):
        for v in range(0, shifts, 8):
            folded.append(fold([each[v + k] for k in (0, 4, 2, 6, 1, 5, 3, 7)], op))
    whole = length.astype(jnp.float32)
    half = shifts // 8
    folded[half:] = [part / whole for part in folded[half:]]
    packed = jnp.concatenate(folded, axis=0).T
    for q in range(nq):
        send[q, :own, :2 * shifts] = packed[q * own:(q + 1) * own]

    def result_copy(i):
        target = other(i, query)
        return pltpu.make_async_remote_copy(
            src_ref=send.at[target],
            dst_ref=recv.at[query],
            send_sem=query_send.at[i],
            recv_sem=query_recv.at[query],
            device_id={"query": target},
            device_id_type=MESH,
        )

    def result_wait(i):
        source = other(i, query)
        pltpu.make_async_remote_copy(
            src_ref=send.at[source],
            dst_ref=recv.at[source],
            send_sem=query_send.at[i],
            recv_sem=query_recv.at[source],
            device_id={"query": source},
            device_id_type=MESH,
        ).wait_recv()

    @pl.when(jnp.logical_not(leads))
    def _():
        pl.semaphore_wait(go, 1)

    for i in range(nq - 1):
        result_copy(i).start()
    for h in range(parts):
        for i in range(nb - 1):
            theo_copy(band, other(i, band), h).wait_send()
    for i in range(nq - 1):
        result_copy(i).wait_send()
    mine = send[query]
    top, mean = mine, mine
    for i in range(nq - 1):
        result_wait(i)
        part = recv[other(i, query)]
        top = jnp.maximum(top, part)
        mean = mean + part
    out_ref[0] = top[:own, :shifts]
    out_ref[1] = pltpu.roll(mean, LANES - shifts, 1)[:own, :shifts]


def local(spectra, theo, offsets, win_lo, win_len):
    nb, nq = lax.axis_size("band"), lax.axis_size("query")
    rows, bins = spectra.shape
    peps = theo.shape[1]
    shifts = offsets.shape[0]
    own = rows // nq
    slots = (own + 7) // 8 * 8
    chunks = nb * peps // 8
    placed = [pltpu.with_memory_space_constraint(x, pltpu.HBM) for x in (spectra, theo, offsets, win_lo, win_len)]
    both = pl.pallas_call(
        functools.partial(kernel, nb, nq),
        out_shape=pltpu.VMEM((2, own, shifts), jnp.float32),
        in_specs=[
            pl.BlockSpec(memory_space=pltpu.HBM),
        ] * 5,
        out_specs=pl.BlockSpec(memory_space=pltpu.VMEM),
        scratch_shapes=[
            pltpu.VMEM((rows, bins + 2 * LANES), jnp.bfloat16),
            pltpu.VMEM((rows, bins), jnp.bfloat16),
            pltpu.VMEM((nb, peps, bins + LANES), jnp.bfloat16),
            pltpu.VMEM((chunks, bins // LANES + 2, 16, LANES), jnp.bfloat16),
            pltpu.VMEM((chunks, 16 * shifts, 2 * rows), jnp.float32),
            pltpu.VMEM((2, BLOCK, BLOCK), jnp.bfloat16),
            pltpu.VMEM((nq, slots, LANES), jnp.float32),
            pltpu.VMEM((nq, slots, LANES), jnp.float32),
            pltpu.SMEM((shifts,), jnp.int32),
            pltpu.VMEM((rows,), jnp.int32),
            pltpu.VMEM((rows,), jnp.int32),
            pltpu.SemaphoreType.DMA((3,)),
            pltpu.SemaphoreType.DMA((bins // (BLOCK * BOX_BLOCKS),)),
            pltpu.SemaphoreType.DMA,
            pltpu.SemaphoreType.DMA((nb, len(CUTS))),
            pltpu.SemaphoreType.DMA((nb, len(CUTS))),
            pltpu.SemaphoreType.DMA((nq,)),
            pltpu.SemaphoreType.DMA((nq,)),
            pltpu.SemaphoreType.REGULAR((nb,)),
            pltpu.SemaphoreType.REGULAR,
        ],
        compiler_params=pltpu.CompilerParams(
            collective_id=0, has_side_effects=True, vmem_limit_bytes=40 * 2**20
        ),
        name="shifted_scores",
    )(*placed)
    return both[0], both[1]


def solution(mesh):
    placed = (P("band", None), P("query", "band", None), P(), P("band"), P("band"))
    return jax.shard_map(
        local,
        mesh=mesh,
        in_specs=placed,
        out_specs=(P(("band", "query"), None), P(("band", "query"), None)),
        check_vma=False,
    )
```

```python
import functools

import jax
import jax.numpy as jnp
from jax import lax
from jax.experimental import pallas as pl
from jax.experimental.pallas import tpu as pltpu
from jax.sharding import PartitionSpec as P

BG_HALF = 75
SHIFT_MAX = 128
LANES = 128
BLOCK = 256
BOX_BLOCKS = 16
CUTS = (2, 9, 20)
MEET = 1
MESH = pl.DeviceIdType.MESH


def box_tables():
    row = lax.broadcasted_iota(jnp.int32, (BLOCK, BLOCK), 0)
    target = lax.broadcasted_iota(jnp.int32, (BLOCK, BLOCK), 1)
    gap = row - target
    middle = (jnp.abs(gap) <= BG_HALF) & (gap != 0)
    side_gap = jnp.where(row < LANES, row - LANES, row + LANES) - target
    side = jnp.abs(side_gap) <= BG_HALF
    return middle.astype(jnp.float32).astype(jnp.bfloat16), side.astype(jnp.float32).astype(jnp.bfloat16)


def other(i, me):
    return i + (i >= me).astype(jnp.int32)


def kernel(
    nb, nq,
    spectra_ref, theo_ref, offsets_hbm, lo_hbm, len_hbm,
    out_ref,
    spec, corr, gathered, pairs, sums, tables, send, recv,
    offsets_ref, lo_ref, len_ref, small_sem, spec_sem, own_sem, band_send, band_recv, query_send, query_recv, arrived, go,
):
    rows, bins = spectra_ref.shape
    peps = theo_ref.shape[1]
    shifts = offsets_hbm.shape[0]
    own = rows // nq
    blocks = bins // LANES
    per_chunk = 8 // peps
    chunks = nb * peps // 8
    width = BLOCK * BOX_BLOCKS
    box_steps = bins // width
    band = lax.axis_index("band")
    query = lax.axis_index("query")
    cuts = [0] + [blocks * cut // CUTS[-1] // 8 * 8 for cut in CUTS]
    parts = len(CUTS)

    last = nb - 1
    leads, closes = band == 0, band == last
    between = jnp.logical_not(leads | closes)
    barrier = pltpu.get_barrier_semaphore()

    def signal(semaphore, axis, index):
        pl.semaphore_signal(semaphore, inc=1, device_id={axis: index}, device_id_type=MESH)

    @pl.when(jnp.logical_not(closes))
    def _():
        signal(barrier, "band", last)

    @pl.when(leads)
    def _():
        for b in range(1, last):
            signal(barrier, "band", b)

    def spec_copy(i):
        start = pl.multiple_of(i * width, width)
        return pltpu.make_async_copy(
            spectra_ref.at[:, pl.ds(start, width)],
            spec.at[:, pl.ds(pl.multiple_of(start + LANES, LANES), width)],
            spec_sem.at[i],
        )

    own_copy = pltpu.make_async_copy(theo_ref.at[0], gathered.at[band, :, pl.ds(0, bins)], own_sem)
    small = [
        pltpu.make_async_copy(source, target, small_sem.at[i])
        for i, (source, target) in enumerate(
            [(offsets_hbm, offsets_ref), (lo_hbm, lo_ref), (len_hbm, len_ref)]
        )
    ]

    def theo_copy(source, target, h):
        at = pl.ds(cuts[h] * LANES, (cuts[h + 1] - cuts[h]) * LANES)
        return pltpu.make_async_remote_copy(
            src_ref=theo_ref.at[0, :, at],
            dst_ref=gathered.at[source, :, at],
            send_sem=band_send.at[target, h],
            recv_sem=band_recv.at[source, h],
            device_id={"band": target},
            device_id_type=MESH,
        )

    def theo_start(targets):
        for h in range(parts):
            for target in targets:
                theo_copy(band, target, h).start()

    for i in range(box_steps):
        spec_copy(i).start()
    own_copy.start()
    for copy in small:
        copy.start()

    @pl.when(between)
    def _():
        pl.semaphore_wait(barrier, 1)
        signal(arrived.at[band], "band", 0)
        theo_start([0])

    @pl.when(closes)
    def _():
        pl.semaphore_wait(barrier, last)
        for b in range(last):
            signal(arrived.at[last], "band", b)
        theo_start(list(range(last - 1)))


    @pl.when(between)
    def _():
        pl.semaphore_wait(arrived.at[last], 1)
        theo_start([last] + [other(i + 1, band) for i in range(nb - 3)])


    @pl.when(leads)
    def _():
        for b in range(1, last):
            pl.semaphore_wait(arrived.at[b], 1)
        theo_start(list(range(1, last)))
        pl.semaphore_wait(arrived.at[last], 1)
        theo_start([last])
        for i in range(nq - 1):
            signal(barrier, "query", other(i, query))

    spec[:, :LANES] = jnp.zeros((rows, LANES), spec.dtype)
    spec[:, LANES + bins:] = jnp.zeros((rows, LANES), spec.dtype)
    tables[0], tables[1] = box_tables()
    send[...] = jnp.zeros_like(send)
    gathered[:, :, bins:] = jnp.zeros((nb, peps, LANES), gathered.dtype)
    for c in range(chunks):
        pairs[c, blocks + 1] = jnp.zeros((16, LANES), pairs.dtype)
    for copy in small:
        copy.wait()

    spec_copy(0).wait()

    @pl.when(closes)
    def _():
        theo_start([last - 1])

    @pl.loop(0, box_steps)
    def _(i):
        @pl.when(i + 1 < box_steps)
        def _():
            spec_copy(i + 1).wait()

        start = pl.multiple_of(i * width, width)
        middles, sides = [], []
        for j in range(BOX_BLOCKS):
            at = start + j * BLOCK
            before = spec[:, pl.ds(pl.multiple_of(at, LANES), LANES)]
            middles.append(spec[:, pl.ds(pl.multiple_of(at + LANES, LANES), BLOCK)])
            after = spec[:, pl.ds(pl.multiple_of(at + LANES + BLOCK, LANES), LANES)]
            sides.append(jnp.concatenate([before, after], axis=1))
        box = jnp.dot(jnp.concatenate(middles, axis=0), tables[0], preferred_element_type=jnp.float32)
        box += jnp.dot(jnp.concatenate(sides, axis=0), tables[1], preferred_element_type=jnp.float32)
        for j in range(BOX_BLOCKS):
            level = box[j * rows:(j + 1) * rows] * (1.0 / (2.0 * BG_HALF))
            fixed = middles[j].astype(jnp.float32) - level
            corr[:, pl.ds(pl.multiple_of(start + j * BLOCK, BLOCK), BLOCK)] = fixed.astype(jnp.bfloat16)

    own_copy.wait()
    lane = lax.broadcasted_iota(jnp.int32, (16, LANES), 1).astype(jnp.float32).astype(jnp.bfloat16)
    ahead = [SHIFT_MAX - offsets_ref[k] for k in range(shifts)]
    skip = [a // LANES for a in ahead]
    rest = [a % LANES for a in ahead]
    turn = [(LANES - r) % LANES for r in rest]
    edge = [jnp.full((16, LANES), r.astype(jnp.float32)).astype(jnp.bfloat16) for r in rest]
    wide = shifts * 16

    def read_blocks(c, first):
        at = pl.ds(pl.multiple_of(first * LANES, LANES), 9 * LANES)
        rows_of = [gathered[c * per_chunk + j, :, at].astype(jnp.float32) for j in range(per_chunk)]
        whole = jnp.concatenate(rows_of, axis=0)
        return [whole[:, t * LANES:(t + 1) * LANES] for t in range(9)]

    def pair(c, g):
        found = read_blocks(c, g * 8)
        for t in range(8):
            pairs[c, g * 8 + t + 1] = jnp.concatenate(found[t:t + 2], axis=0).astype(jnp.bfloat16)

    def span(c, first, last):
        columns, evens, odds = [], [], []
        for j in range(first, last, 2):
            turned = []
            for k in range(shifts):
                near = pairs[c, j + skip[k]]
                far = pairs[c, j + skip[k] + 1]
                turned.append(pltpu.roll(jnp.where(lane < edge[k], far, near), turn[k], 1))
            columns.append(jnp.concatenate(turned, axis=0))
            evens.append(corr[:, j * LANES:(j + 1) * LANES])
            odds.append(corr[:, (j + 1) * LANES:(j + 2) * LANES])
        shifted = jnp.concatenate(columns, axis=1)
        piece = jnp.concatenate(
            [jnp.concatenate(evens, axis=1), jnp.concatenate(odds, axis=1)], axis=0
        )
        return lax.dot_general(
            shifted, piece, (((1,), (1,)), ((), ())), preferred_element_type=jnp.float32
        )

    group_from = block_from = 0
    for h in range(parts):
        for i in range(nb - 1):
            theo_copy(other(i, band), other(i, band), h).wait_recv()
        if h < parts - 1:
            group_to = (cuts[h + 1] - 1) // 8
            block_to = (group_to * 8 - 1) // 4 * 4
        else:
            group_to, block_to = blocks // 8, blocks

        def work(c):
            if h == 0:
                start = read_blocks(c, 0)[0]
                pairs[c, 0] = jnp.concatenate([jnp.zeros_like(start), start], axis=0).astype(jnp.bfloat16)
            pl.loop(group_from, group_to, unroll=True)(functools.partial(pair, c))
            found = span(c, block_from, block_to)
            sums[c] = found if h == 0 else sums[c] + found

        if chunks == 1:
            work(0)
        else:
            pl.loop(0, chunks)(work)
        group_from, block_from = group_to, block_to

        if h == MEET:
            @pl.when(leads)
            def _():
                pl.semaphore_wait(barrier, nq - 1)
                for b in range(1, nb):
                    signal(go, "band", b)

    row = lax.broadcasted_iota(jnp.int32, (8, rows), 0)
    lo = jnp.broadcast_to(lo_ref[...].reshape(1, rows), (8, rows))
    length = jnp.broadcast_to(len_ref[...].reshape(1, rows), (8, rows))
    best = [jnp.full((8, rows), -jnp.inf, jnp.float32)] * shifts
    total = [jnp.zeros((8, rows), jnp.float32)] * shifts
    for c in range(chunks):
        number = row + (query * (chunks * 8) + c * 8)
        inside = (number >= lo) & (number < lo + length)
        for k in range(shifts):
            scores = sums[c, 16 * k:16 * k + 8, :rows] + sums[c, 16 * k + 8:16 * k + 16, rows:]
            best[k] = jnp.maximum(best[k], jnp.where(inside, scores, -jnp.inf))
            total[k] = total[k] + jnp.where(inside, scores, 0.0)

    def fold(each, op):
        for reach in (4, 2, 1):
            upper = (row // reach) % 2 == 1
            merged = []
            for n in range(0, len(each), 2):
                moved = jnp.where(upper, each[n], each[n + 1])
                moved = jnp.where(upper, pltpu.roll(moved, reach, 0), pltpu.roll(moved, 8 - reach, 0))
                merged.append(op(jnp.where(upper, each[n + 1], each[n]), moved))
            each = merged
        return each[0]

    folded = []
    for each, op in ((best, jnp.maximum), (total, jnp.add)):
        for v in range(0, shifts, 8):
            folded.append(fold([each[v + k] for k in (0, 4, 2, 6, 1, 5, 3, 7)], op))
    whole = length.astype(jnp.float32)
    half = shifts // 8
    folded[half:] = [part / whole for part in folded[half:]]
    packed = jnp.concatenate(folded, axis=0).T
    for q in range(nq):
        send[q, :own, :2 * shifts] = packed[q * own:(q + 1) * own]

    def result_copy(i):
        target = other(i, query)
        return pltpu.make_async_remote_copy(
            src_ref=send.at[target],
            dst_ref=recv.at[query],
            send_sem=query_send.at[i],
            recv_sem=query_recv.at[query],
            device_id={"query": target},
            device_id_type=MESH,
        )

    def result_wait(i):
        source = other(i, query)
        pltpu.make_async_remote_copy(
            src_ref=send.at[source],
            dst_ref=recv.at[source],
            send_sem=query_send.at[i],
            recv_sem=query_recv.at[source],
            device_id={"query": source},
            device_id_type=MESH,
        ).wait_recv()

    @pl.when(jnp.logical_not(leads))
    def _():
        pl.semaphore_wait(go, 1)

    for i in range(nq - 1):
        result_copy(i).start()
    for h in range(parts):
        for i in range(nb - 1):
            theo_copy(band, other(i, band), h).wait_send()
    for i in range(nq - 1):
        result_copy(i).wait_send()
    mine = send[query]
    top, mean = mine, mine
    for i in range(nq - 1):
        result_wait(i)
        part = recv[other(i, query)]
        top = jnp.maximum(top, part)
        mean = mean + part
    out_ref[0] = top[:own, :shifts]
    out_ref[1] = pltpu.roll(mean, LANES - shifts, 1)[:own, :shifts]


def local(spectra, theo, offsets, win_lo, win_len):
    nb, nq = lax.axis_size("band"), lax.axis_size("query")
    rows, bins = spectra.shape
    peps = theo.shape[1]
    shifts = offsets.shape[0]
    own = rows // nq
    slots = (own + 7) // 8 * 8
    chunks = nb * peps // 8
    placed = [pltpu.with_memory_space_constraint(x, pltpu.HBM) for x in (spectra, theo, offsets, win_lo, win_len)]
    both = pl.pallas_call(
        functools.partial(kernel, nb, nq),
        out_shape=pltpu.VMEM((2, own, shifts), jnp.float32),
        in_specs=[
            pl.BlockSpec(memory_space=pltpu.HBM),
        ] * 5,
        out_specs=pl.BlockSpec(memory_space=pltpu.VMEM),
        scratch_shapes=[
            pltpu.VMEM((rows, bins + 2 * LANES), jnp.bfloat16),
            pltpu.VMEM((rows, bins), jnp.bfloat16),
            pltpu.VMEM((nb, peps, bins + LANES), jnp.bfloat16),
            pltpu.VMEM((chunks, bins // LANES + 2, 16, LANES), jnp.bfloat16),
            pltpu.VMEM((chunks, 16 * shifts, 2 * rows), jnp.float32),
            pltpu.VMEM((2, BLOCK, BLOCK), jnp.bfloat16),
            pltpu.VMEM((nq, slots, LANES), jnp.float32),
            pltpu.VMEM((nq, slots, LANES), jnp.float32),
            pltpu.SMEM((shifts,), jnp.int32),
            pltpu.VMEM((rows,), jnp.int32),
            pltpu.VMEM((rows,), jnp.int32),
            pltpu.SemaphoreType.DMA((3,)),
            pltpu.SemaphoreType.DMA((bins // (BLOCK * BOX_BLOCKS),)),
            pltpu.SemaphoreType.DMA,
            pltpu.SemaphoreType.DMA((nb, len(CUTS))),
            pltpu.SemaphoreType.DMA((nb, len(CUTS))),
            pltpu.SemaphoreType.DMA((nq,)),
            pltpu.SemaphoreType.DMA((nq,)),
            pltpu.SemaphoreType.REGULAR((nb,)),
            pltpu.SemaphoreType.REGULAR,
        ],
        compiler_params=pltpu.CompilerParams(
            collective_id=0, has_side_effects=True, vmem_limit_bytes=40 * 2**20
        ),
        name="shifted_scores",
    )(*placed)
    return both[0], both[1]


def solution(mesh):
    placed = (P("band", None), P("query", "band", None), P(), P("band"), P("band"))
    return jax.shard_map(
        local,
        mesh=mesh,
        in_specs=placed,
        out_specs=(P(("band", "query"), None), P(("band", "query"), None)),
        check_vma=False,
    )
```

```python
import functools

import jax
import jax.numpy as jnp
from jax import lax
from jax.experimental import pallas as pl
from jax.experimental.pallas import tpu as pltpu
from jax.sharding import PartitionSpec as P

BG_HALF = 75
SHIFT_MAX = 128
LANES = 128
BLOCK = 256
BOX_BLOCKS = 16
CUTS = (2, 8, 20)
MEET = 1
MESH = pl.DeviceIdType.MESH


def box_tables():
    row = lax.broadcasted_iota(jnp.int32, (BLOCK, BLOCK), 0)
    target = lax.broadcasted_iota(jnp.int32, (BLOCK, BLOCK), 1)
    gap = row - target
    middle = (jnp.abs(gap) <= BG_HALF) & (gap != 0)
    side_gap = jnp.where(row < LANES, row - LANES, row + LANES) - target
    side = jnp.abs(side_gap) <= BG_HALF
    return middle.astype(jnp.float32).astype(jnp.bfloat16), side.astype(jnp.float32).astype(jnp.bfloat16)


def other(i, me):
    return i + (i >= me).astype(jnp.int32)


def kernel(
    nb, nq,
    spectra_ref, theo_ref, offsets_hbm, lo_hbm, len_hbm,
    out_ref,
    spec, corr, gathered, pairs, sums, tables, send, recv,
    offsets_ref, lo_ref, len_ref, small_sem, spec_sem, own_sem, band_send, band_recv, query_send, query_recv, arrived, go,
):
    rows, bins = spectra_ref.shape
    peps = theo_ref.shape[1]
    shifts = offsets_hbm.shape[0]
    own = rows // nq
    blocks = bins // LANES
    per_chunk = 8 // peps
    chunks = nb * peps // 8
    width = BLOCK * BOX_BLOCKS
    box_steps = bins // width
    band = lax.axis_index("band")
    query = lax.axis_index("query")
    cuts = [0] + [blocks * cut // CUTS[-1] // 8 * 8 for cut in CUTS]
    parts = len(CUTS)

    last = nb - 1
    leads, closes = band == 0, band == last
    between = jnp.logical_not(leads | closes)
    barrier = pltpu.get_barrier_semaphore()

    def signal(semaphore, axis, index):
        pl.semaphore_signal(semaphore, inc=1, device_id={axis: index}, device_id_type=MESH)

    @pl.when(jnp.logical_not(closes))
    def _():
        signal(barrier, "band", last)

    @pl.when(leads)
    def _():
        for b in range(1, last):
            signal(barrier, "band", b)

    def spec_copy(i):
        start = pl.multiple_of(i * width, width)
        return pltpu.make_async_copy(
            spectra_ref.at[:, pl.ds(start, width)],
            spec.at[:, pl.ds(pl.multiple_of(start + LANES, LANES), width)],
            spec_sem.at[i],
        )

    own_copy = pltpu.make_async_copy(theo_ref.at[0], gathered.at[band, :, pl.ds(0, bins)], own_sem)
    small = [
        pltpu.make_async_copy(source, target, small_sem.at[i])
        for i, (source, target) in enumerate(
            [(offsets_hbm, offsets_ref), (lo_hbm, lo_ref), (len_hbm, len_ref)]
        )
    ]

    def theo_copy(source, target, h):
        at = pl.ds(cuts[h] * LANES, (cuts[h + 1] - cuts[h]) * LANES)
        return pltpu.make_async_remote_copy(
            src_ref=theo_ref.at[0, :, at],
            dst_ref=gathered.at[source, :, at],
            send_sem=band_send.at[target, h],
            recv_sem=band_recv.at[source, h],
            device_id={"band": target},
            device_id_type=MESH,
        )

    def theo_start(targets):
        for h in range(parts):
            for target in targets:
                theo_copy(band, target, h).start()

    for i in range(box_steps):
        spec_copy(i).start()
    own_copy.start()
    for copy in small:
        copy.start()

    @pl.when(between)
    def _():
        pl.semaphore_wait(barrier, 1)
        signal(arrived.at[band], "band", 0)
        theo_start([0])

    @pl.when(closes)
    def _():
        pl.semaphore_wait(barrier, last)
        for b in range(last):
            signal(arrived.at[last], "band", b)
        theo_start([0])
        theo_start(list(range(1, last - 1)))


    @pl.when(between)
    def _():
        pl.semaphore_wait(arrived.at[last], 1)
        theo_start([last] + [other(i + 1, band) for i in range(nb - 3)])


    @pl.when(leads)
    def _():
        for b in range(1, last):
            pl.semaphore_wait(arrived.at[b], 1)
        theo_start(list(range(1, last)))
        pl.semaphore_wait(arrived.at[last], 1)
        theo_start([last])
        for i in range(nq - 1):
            signal(barrier, "query", other(i, query))

    spec[:, :LANES] = jnp.zeros((rows, LANES), spec.dtype)
    spec[:, LANES + bins:] = jnp.zeros((rows, LANES), spec.dtype)
    tables[0], tables[1] = box_tables()
    send[...] = jnp.zeros_like(send)
    gathered[:, :, bins:] = jnp.zeros((nb, peps, LANES), gathered.dtype)
    for c in range(chunks):
        pairs[c, blocks + 1] = jnp.zeros((16, LANES), pairs.dtype)
    for copy in small:
        copy.wait()

    spec_copy(0).wait()

    @pl.when(closes)
    def _():
        theo_start([last - 1])

    @pl.loop(0, box_steps)
    def _(i):
        @pl.when(i + 1 < box_steps)
        def _():
            spec_copy(i + 1).wait()

        start = pl.multiple_of(i * width, width)
        middles, sides = [], []
        for j in range(BOX_BLOCKS):
            at = start + j * BLOCK
            before = spec[:, pl.ds(pl.multiple_of(at, LANES), LANES)]
            middles.append(spec[:, pl.ds(pl.multiple_of(at + LANES, LANES), BLOCK)])
            after = spec[:, pl.ds(pl.multiple_of(at + LANES + BLOCK, LANES), LANES)]
            sides.append(jnp.concatenate([before, after], axis=1))
        box = jnp.dot(jnp.concatenate(middles, axis=0), tables[0], preferred_element_type=jnp.float32)
        box += jnp.dot(jnp.concatenate(sides, axis=0), tables[1], preferred_element_type=jnp.float32)
        for j in range(BOX_BLOCKS):
            level = box[j * rows:(j + 1) * rows] * (1.0 / (2.0 * BG_HALF))
            fixed = middles[j].astype(jnp.float32) - level
            corr[:, pl.ds(pl.multiple_of(start + j * BLOCK, BLOCK), BLOCK)] = fixed.astype(jnp.bfloat16)

    own_copy.wait()
    lane = lax.broadcasted_iota(jnp.int32, (16, LANES), 1).astype(jnp.float32).astype(jnp.bfloat16)
    ahead = [SHIFT_MAX - offsets_ref[k] for k in range(shifts)]
    skip = [a // LANES for a in ahead]
    rest = [a % LANES for a in ahead]
    turn = [(LANES - r) % LANES for r in rest]
    edge = [jnp.full((16, LANES), r.astype(jnp.float32)).astype(jnp.bfloat16) for r in rest]
    wide = shifts * 16

    def read_blocks(c, first):
        at = pl.ds(pl.multiple_of(first * LANES, LANES), 9 * LANES)
        rows_of = [gathered[c * per_chunk + j, :, at].astype(jnp.float32) for j in range(per_chunk)]
        whole = jnp.concatenate(rows_of, axis=0)
        return [whole[:, t * LANES:(t + 1) * LANES] for t in range(9)]

    def pair(c, g):
        found = read_blocks(c, g * 8)
        for t in range(8):
            pairs[c, g * 8 + t + 1] = jnp.concatenate(found[t:t + 2], axis=0).astype(jnp.bfloat16)

    def span(c, first, last):
        columns, evens, odds = [], [], []
        for j in range(first, last, 2):
            turned = []
            for k in range(shifts):
                near = pairs[c, j + skip[k]]
                far = pairs[c, j + skip[k] + 1]
                turned.append(pltpu.roll(jnp.where(lane < edge[k], far, near), turn[k], 1))
            columns.append(jnp.concatenate(turned, axis=0))
            evens.append(corr[:, j * LANES:(j + 1) * LANES])
            odds.append(corr[:, (j + 1) * LANES:(j + 2) * LANES])
        shifted = jnp.concatenate(columns, axis=1)
        piece = jnp.concatenate(
            [jnp.concatenate(evens, axis=1), jnp.concatenate(odds, axis=1)], axis=0
        )
        return lax.dot_general(
            shifted, piece, (((1,), (1,)), ((), ())), preferred_element_type=jnp.float32
        )

    group_from = block_from = 0
    for h in range(parts):
        for i in range(nb - 1):
            theo_copy(other(i, band), other(i, band), h).wait_recv()
        if h < parts - 1:
            group_to = (cuts[h + 1] - 1) // 8
            block_to = (group_to * 8 - 1) // 4 * 4
        else:
            group_to, block_to = blocks // 8, blocks

        def work(c):
            if h == 0:
                start = read_blocks(c, 0)[0]
                pairs[c, 0] = jnp.concatenate([jnp.zeros_like(start), start], axis=0).astype(jnp.bfloat16)
            pl.loop(group_from, group_to, unroll=True)(functools.partial(pair, c))
            found = span(c, block_from, block_to)
            sums[c] = found if h == 0 else sums[c] + found

        if chunks == 1:
            work(0)
        else:
            pl.loop(0, chunks)(work)
        group_from, block_from = group_to, block_to

        if h == MEET:
            @pl.when(leads)
            def _():
                pl.semaphore_wait(barrier, nq - 1)
                for b in range(1, nb):
                    signal(go, "band", b)

    row = lax.broadcasted_iota(jnp.int32, (8, rows), 0)
    lo = jnp.broadcast_to(lo_ref[...].reshape(1, rows), (8, rows))
    length = jnp.broadcast_to(len_ref[...].reshape(1, rows), (8, rows))
    best = [jnp.full((8, rows), -jnp.inf, jnp.float32)] * shifts
    total = [jnp.zeros((8, rows), jnp.float32)] * shifts
    for c in range(chunks):
        number = row + (query * (chunks * 8) + c * 8)
        inside = (number >= lo) & (number < lo + length)
        for k in range(shifts):
            scores = sums[c, 16 * k:16 * k + 8, :rows] + sums[c, 16 * k + 8:16 * k + 16, rows:]
            best[k] = jnp.maximum(best[k], jnp.where(inside, scores, -jnp.inf))
            total[k] = total[k] + jnp.where(inside, scores, 0.0)

    def fold(each, op):
        for reach in (4, 2, 1):
            upper = (row // reach) % 2 == 1
            merged = []
            for n in range(0, len(each), 2):
                moved = jnp.where(upper, each[n], each[n + 1])
                moved = jnp.where(upper, pltpu.roll(moved, reach, 0), pltpu.roll(moved, 8 - reach, 0))
                merged.append(op(jnp.where(upper, each[n + 1], each[n]), moved))
            each = merged
        return each[0]

    folded = []
    for each, op in ((best, jnp.maximum), (total, jnp.add)):
        for v in range(0, shifts, 8):
            folded.append(fold([each[v + k] for k in (0, 4, 2, 6, 1, 5, 3, 7)], op))
    whole = length.astype(jnp.float32)
    half = shifts // 8
    folded[half:] = [part / whole for part in folded[half:]]
    packed = jnp.concatenate(folded, axis=0).T
    for q in range(nq):
        send[q, :own, :2 * shifts] = packed[q * own:(q + 1) * own]

    def result_copy(i):
        target = other(i, query)
        return pltpu.make_async_remote_copy(
            src_ref=send.at[target],
            dst_ref=recv.at[query],
            send_sem=query_send.at[i],
            recv_sem=query_recv.at[query],
            device_id={"query": target},
            device_id_type=MESH,
        )

    def result_wait(i):
        source = other(i, query)
        pltpu.make_async_remote_copy(
            src_ref=send.at[source],
            dst_ref=recv.at[source],
            send_sem=query_send.at[i],
            recv_sem=query_recv.at[source],
            device_id={"query": source},
            device_id_type=MESH,
        ).wait_recv()

    @pl.when(jnp.logical_not(leads))
    def _():
        pl.semaphore_wait(go, 1)

    for i in range(nq - 1):
        result_copy(i).start()
    for h in range(parts):
        for i in range(nb - 1):
            theo_copy(band, other(i, band), h).wait_send()
    for i in range(nq - 1):
        result_copy(i).wait_send()
    mine = send[query]
    top, mean = mine, mine
    for i in range(nq - 1):
        result_wait(i)
        part = recv[other(i, query)]
        top = jnp.maximum(top, part)
        mean = mean + part
    out_ref[0] = top[:own, :shifts]
    out_ref[1] = pltpu.roll(mean, LANES - shifts, 1)[:own, :shifts]


def local(spectra, theo, offsets, win_lo, win_len):
    nb, nq = lax.axis_size("band"), lax.axis_size("query")
    rows, bins = spectra.shape
    peps = theo.shape[1]
    shifts = offsets.shape[0]
    own = rows // nq
    slots = (own + 7) // 8 * 8
    chunks = nb * peps // 8
    placed = [pltpu.with_memory_space_constraint(x, pltpu.HBM) for x in (spectra, theo, offsets, win_lo, win_len)]
    both = pl.pallas_call(
        functools.partial(kernel, nb, nq),
        out_shape=pltpu.VMEM((2, own, shifts), jnp.float32),
        in_specs=[
            pl.BlockSpec(memory_space=pltpu.HBM),
        ] * 5,
        out_specs=pl.BlockSpec(memory_space=pltpu.VMEM),
        scratch_shapes=[
            pltpu.VMEM((rows, bins + 2 * LANES), jnp.bfloat16),
            pltpu.VMEM((rows, bins), jnp.bfloat16),
            pltpu.VMEM((nb, peps, bins + LANES), jnp.bfloat16),
            pltpu.VMEM((chunks, bins // LANES + 2, 16, LANES), jnp.bfloat16),
            pltpu.VMEM((chunks, 16 * shifts, 2 * rows), jnp.float32),
            pltpu.VMEM((2, BLOCK, BLOCK), jnp.bfloat16),
            pltpu.VMEM((nq, slots, LANES), jnp.float32),
            pltpu.VMEM((nq, slots, LANES), jnp.float32),
            pltpu.SMEM((shifts,), jnp.int32),
            pltpu.VMEM((rows,), jnp.int32),
            pltpu.VMEM((rows,), jnp.int32),
            pltpu.SemaphoreType.DMA((3,)),
            pltpu.SemaphoreType.DMA((bins // (BLOCK * BOX_BLOCKS),)),
            pltpu.SemaphoreType.DMA,
            pltpu.SemaphoreType.DMA((nb, len(CUTS))),
            pltpu.SemaphoreType.DMA((nb, len(CUTS))),
            pltpu.SemaphoreType.DMA((nq,)),
            pltpu.SemaphoreType.DMA((nq,)),
            pltpu.SemaphoreType.REGULAR((nb,)),
            pltpu.SemaphoreType.REGULAR,
        ],
        compiler_params=pltpu.CompilerParams(
            collective_id=0, has_side_effects=True, vmem_limit_bytes=40 * 2**20
        ),
        name="shifted_scores",
    )(*placed)
    return both[0], both[1]


def solution(mesh):
    placed = (P("band", None), P("query", "band", None), P(), P("band"), P("band"))
    return jax.shard_map(
        local,
        mesh=mesh,
        in_specs=placed,
        out_specs=(P(("band", "query"), None), P(("band", "query"), None)),
        check_vma=False,
    )
```
